32 devices in a mesh: groups: 2 (over x), ty: 8 (over z, y), tx: 2 (over core).
Axes of the slice: x: 2, y: 2, z: 4, core: 2. Of those that a mesh axis runs over, the one named last changes fastest.
Arguments:
- fields: bfloat16 [6, 2048, 1024], P(None, ('groups', 'ty'), 'tx'), parts along dimension 1, may hold values from -8 to 8
- weights: bfloat16 [2048, 1024], P(('groups', 'ty'), 'tx'), parts along dimension 0, may hold values from 0.049804688 to 0.94921875
- source_tile: int32 [16, 8, 2], P(('groups', 'ty'), 'tx'), parts along dimension 0, may hold values from 0 to 15, as said below
- source_block: int32 [16, 8, 2], P(('groups', 'ty'), 'tx'), parts along dimension 0, may hold values from 0 to 3
- coupling: bfloat16 [6, 6], replicated, may hold values from -2.5 to 2.5
- driver: float32 [6, 128, 128], replicated, may hold values from -48 to 48
- relaxation: float32 [6, 128, 128], replicated, may hold values from 0.05 to 0.6
Outputs:
- nudged: float32 [6, 2048, 1024], P(None, ('groups', 'ty'), 'tx'), parts along dimension 1
The draws below stay inside these ranges and needn't reach their ends.
There are 2 independent parts, one for each index of `groups`. The reference program is written for one: setup_inputs(seed, part) draws one part's arguments, and reference() takes and returns one part's arrays. A program takes and returns all parts, laid end to end along the dimension named above; an argument that names none is the same for every part. Nothing has to cross between parts.
Inputs may be any that keep to these rules, and one draw needn't show every extreme that they name: `source_tile`: the two sources of a block lie in the same block row, the second one block column east of the first (wrapping around the domain). Among the 8 requests of one tile, no tile row of owners is named more than 4 times, and in every tile some owner tile is named exactly 4 times.
All inputs are finite; a program needn't handle non-finite values.
Results may differ from the reference program's by a relative error of at most 0.0003.
Values may be sent and summed in bfloat16 or wider, within the bound.
No kernel may reach another device: no remote copies, remote signals or barrier semaphores. Data moves between devices by JAX's collectives and lax.ppermute only.
A program may use at most 128 MiB of HBM per device.

```python
import math
import jax
import jax.numpy as jnp
from jax import lax

FIELDS = 6
BS = 128
KSRC = 2
KMAX = 64
MODES = 128
TH = 128
TW = 512
BX = 4
NY = 1024
NX = 1024
NBY = 8
NBX = 8
N_TY = 8
N_TX = 2


def request_table(key):
    base = jax.random.fold_in(key, 7303)
    key_wy, key_wx, key_pair, key_far = jax.random.split(base, 4)
    wind_y = jax.random.randint(key_wy, (N_TY, N_TX), -3, 4)
    wind_x = jax.random.randint(key_wx, (N_TY, N_TX), -6, 7)
    far_row = jax.random.randint(jax.random.fold_in(key_far, 1), (), 0, N_TY)
    far_col = jax.random.randint(jax.random.fold_in(key_far, 2), (), 0, N_TX)
    tile_row = jnp.arange(N_TY, dtype=jnp.int32)[:, None, None]
    tile_col = jnp.arange(N_TX, dtype=jnp.int32)[None, :, None]
    is_far = (tile_row[..., 0] == far_row) & (tile_col[..., 0] == far_col)
    wind_y = jnp.where(is_far, N_TY // 2, wind_y)
    wind_x = jnp.where(is_far, 0, wind_x)
    offset = 2 * jax.random.randint(key_pair, (N_TY, N_TX), 0, BX // 2)
    column = jnp.arange(BX, dtype=jnp.int32)
    pair_row = (column[None, None, :] + offset[..., None]) % BX // 2 - BX // 4
    source_row = (tile_row + wind_y[..., None] + pair_row) % NBY
    first_col = (tile_col * BX + column[None, None, :] + wind_x[..., None]) % NBX
    both_cols = jnp.stack([first_col, (first_col + 1) % NBX], axis=-1)
    both_rows = jnp.broadcast_to(source_row[..., None], both_cols.shape)
    owners = both_rows * N_TX + both_cols // BX
    blocks = both_cols % BX
    return (owners.reshape(NBY, NBX, KSRC).astype(jnp.int32), blocks.reshape(NBY, NBX, KSRC).astype(jnp.int32))


def draw_source_tile(key, part):
    return request_table(key)[0]


def draw_source_block(key, part):
    return request_table(key)[1]


def draw_fields(key, part):
    key_rough, key_scale, key_ky, key_kx, key_py, key_px, key_amp = jax.random.split(jax.random.fold_in(key, 911), 7)
    spread = jnp.exp(jax.random.uniform(key_scale, (FIELDS, NY, NX), jnp.float32, -0.7, 0.7))
    rough = jnp.clip(jax.random.normal(key_rough, (FIELDS, NY, NX), jnp.float32), -3.0, 3.0) * spread
    wave_y = jax.random.randint(key_ky, (FIELDS, 6), 0, 9).astype(jnp.float32)
    wave_x = jax.random.randint(key_kx, (FIELDS, 6), 0, 9).astype(jnp.float32)
    phase_y = jax.random.uniform(key_py, (FIELDS, 6), jnp.float32, -math.pi, math.pi)
    phase_x = jax.random.uniform(key_px, (FIELDS, 6), jnp.float32, -math.pi, math.pi)
    amplitude = jax.random.uniform(key_amp, (FIELDS, 6), jnp.float32, 0.2, 0.5)
    rows_f = jnp.arange(NY, dtype=jnp.float32)
    cols_f = jnp.arange(NX, dtype=jnp.float32)
    angle_y = 2.0 * math.pi * wave_y[..., None] * rows_f / NY + phase_y[..., None]
    angle_x = 2.0 * math.pi * wave_x[..., None] * cols_f / NX + phase_x[..., None]
    smooth = jnp.einsum('fwy,fwx->fyx', amplitude[..., None] * jnp.cos(angle_y), jnp.cos(angle_x))
    smooth = smooth - jnp.einsum('fwy,fwx->fyx', amplitude[..., None] * jnp.sin(angle_y), jnp.sin(angle_x))
    return jnp.clip(rough + smooth, -8.0, 8.0).astype(jnp.bfloat16)


def steps_of(key, shape, shards, low, largest):
    gain, own = 1.0, jax.random.fold_in(key, 6)
    for dim, shards_of in shards:
        draws = jnp.exp(jax.random.uniform(jax.random.fold_in(own, dim), (shards_of,), jnp.float32, low / len(shards), largest / len(shards)))
        gain = gain * jnp.repeat(draws, shape[dim] // shards_of).reshape([-1 if axis == dim else 1 for axis in range(len(shape))])
    return gain


def gaussian(key, shape, width, limit, kind=jnp.bfloat16):
    array = jax.random.normal(key, shape, jnp.float32) * width
    return jnp.minimum(jnp.maximum(array, -limit), limit).astype(kind)


def setup_inputs(seed: int = 0, part: int = 0) -> dict:
    key_of = jax.random.split(jax.random.key(seed), 8)
    part_keys = jax.random.split(jax.random.fold_in(key_of[7], part), 8)
    fields = draw_fields(jax.random.fold_in(jax.random.fold_in(key_of[7], part), 71), part)
    weights = jnp.clip(0.049804688 + 0.89941406 * jax.random.uniform(part_keys[1], (NY, NX), jnp.float32) ** steps_of(part_keys[1], (NY, NX), ((0, 8), (1, 2)), -0.2, 0.2), 0.049804688, 0.94921875).astype(jnp.bfloat16)
    source_tile = draw_source_tile(jax.random.fold_in(jax.random.fold_in(key_of[7], part), 71), part)
    source_block = draw_source_block(jax.random.fold_in(jax.random.fold_in(key_of[7], part), 71), part)
    coupling = gaussian(key_of[4], (FIELDS, FIELDS), FIELDS ** -0.5, 2.5)
    driver = gaussian(key_of[5], (FIELDS, MODES, MODES), 8.0, 48.0, jnp.float32)
    relaxation = jnp.clip(jax.random.uniform(key_of[6], (FIELDS, MODES, MODES), jnp.float32, 0.05, 0.6), 0.05, 0.6)
    return {"fields": fields, "weights": weights, "source_tile": source_tile, "source_block": source_block, "coupling": coupling, "driver": driver, "relaxation": relaxation}


def wave_basis(offset, extent, period):
    position = offset + jnp.arange(extent, dtype=jnp.int32)
    mode_index = jnp.arange(KMAX, dtype=jnp.int32)
    cos_phase = position[:, None] * mode_index[None, :] % period
    sin_phase = position[:, None] * (mode_index[None, :] + 1) % period
    norming = jnp.where(mode_index == 0, math.sqrt(1.0 / period), math.sqrt(2.0 / period)).astype(jnp.float32)
    cos_part = jnp.cos(2.0 * math.pi * cos_phase.astype(jnp.float32) / period) * norming[None, :]
    sin_part = jnp.sin(2.0 * math.pi * sin_phase.astype(jnp.float32) / period) * math.sqrt(2.0 / period)
    return jnp.concatenate([cos_part, sin_part], axis=1).astype(jnp.float32)

def reference(fields, weights, source_tile, source_block, coupling, driver, relaxation):
    highest = lax.Precision.HIGHEST

    def fetch_block(tile_id, block_id):
        row_start = tile_id // N_TX * TH + block_id // BX * BS
        col_start = tile_id % N_TX * TW + block_id % BX * BS
        return lax.dynamic_slice(fields, (jnp.int32(0), row_start.astype(jnp.int32), col_start.astype(jnp.int32)), (FIELDS, BS, BS))

    def one_row(block_row):
        sources = jax.vmap(jax.vmap(fetch_block))(source_tile[block_row], source_block[block_row])
        row_weights = lax.dynamic_slice_in_dim(weights, (block_row * BS).astype(jnp.int32), BS, 0)
        row_weights = row_weights.reshape(BS, NBX, BS).transpose(1, 0, 2).astype(jnp.float32)
        first = sources[:, 0].astype(jnp.float32)
        second = sources[:, 1].astype(jnp.float32)
        blended = row_weights[:, None] * first + (1.0 - row_weights)[:, None] * second
        return blended.transpose(1, 2, 0, 3).reshape(FIELDS, BS, NX)
    upstream_rows = lax.map(one_row, jnp.arange(NBY, dtype=jnp.int32))
    interpolated = upstream_rows.transpose(1, 0, 2, 3).reshape(FIELDS, NY, NX)
    tendency = jnp.einsum('gf,fyx->gyx', coupling.astype(jnp.float32), fields.astype(jnp.float32), precision=highest)
    upstream = interpolated + tendency
    row_basis = wave_basis(0, NY, NY)
    col_basis = wave_basis(0, NX, NX)
    col_modes = jnp.einsum('fyx,xn->fyn', upstream, col_basis, precision=highest)
    coefficients = jnp.einsum('ym,fyn->fmn', row_basis, col_modes, precision=highest)
    nudge_term = relaxation * (driver - coefficients)
    row_recon = jnp.einsum('ym,fmn->fyn', row_basis, nudge_term, precision=highest)
    correction = jnp.einsum('fyn,xn->fyx', row_recon, col_basis, precision=highest)
    return upstream + correction
```

```python
import functools
import math

import jax
import jax.numpy as jnp
import ml_dtypes
import numpy as np
from jax import lax
from jax.experimental import pallas as pl
from jax.experimental.pallas import tpu as pltpu
from jax.sharding import PartitionSpec as P

BS = 128
KSRC = 2
KMAX = 64
MODES = 2 * KMAX
IDX_ROWS = 16


def wave_table(period):
    position = np.arange(period, dtype=np.int64)[:, None]
    k = np.arange(KMAX, dtype=np.int64)[None, :]
    norm = np.where(k == 0, math.sqrt(1.0 / period), math.sqrt(2.0 / period))
    cos_part = np.cos(2.0 * math.pi * (position * k % period) / period) * norm
    sin_part = np.sin(2.0 * math.pi * (position * (k + 1) % period) / period)
    table = np.concatenate([cos_part, sin_part * math.sqrt(2.0 / period)], axis=1)
    high = table.astype(np.float32).astype(ml_dtypes.bfloat16)
    low = (table - high.astype(np.float64)).astype(np.float32).astype(ml_dtypes.bfloat16)
    return np.concatenate([high, low], axis=1)


def ring_order(mesh):
    axes = mesh.axis_names
    devices = np.moveaxis(np.asarray(mesh.devices), axes.index("ty"), 0)
    row = devices.reshape(devices.shape[0], -1)[:, 0]
    extent = len(row)
    natural = list(range(extent))
    coords = [getattr(d, "coords", None) for d in row]
    if extent < 3 or any(c is None for c in coords):
        return natural
    near = [
        [j for j in natural if sum(abs(a - b) for a, b in zip(coords[i], coords[j])) == 1]
        for i in natural
    ]
    budget = [20000]

    def extend(path):
        budget[0] -= 1
        if budget[0] < 0:
            return None
        if len(path) == extent:
            return path if path[0] in near[path[-1]] else None
        for j in near[path[-1]]:
            if j not in path:
                found = extend(path + [j])
                if found is not None:
                    return found
        return None

    return extend([0]) or natural


def split(x):
    high = x.astype(jnp.bfloat16)
    return high, (x - high.astype(jnp.float32)).astype(jnp.bfloat16)


def dot(a, b, dims=((1,), (0,))):
    return lax.dot_general(a, b, (dims, ((), ())), preferred_element_type=jnp.float32)


def remap_kernel(
    n, per_tile, cols, srow, scol, place, *refs
):
    pieces = refs[:n]
    w_own, w_other, ctab, rtab, mine_ref, send_ref, fld, high, low, modes, sems = refs[n:]
    half = per_tile * BS
    copies = []
    for k in range(n):
        copy = pltpu.make_async_copy(pieces[k], fld.at[place[k]], sems.at[k])
        copy.start()
        copies.append(copy)
    for copy in copies:
        copy.wait()
    my_col = place[n]

    def blend_row(k, first):
        row0 = pl.multiple_of(place[k] * BS, BS)
        for h, w_ref in ((0, w_own), (1, w_other)):
            at = my_col if h == 0 else 1 - my_col
            for b in range(per_tile):
                e = ((k * 2 + h) * per_tile + b) * KSRC
                s0 = fld[srow[e], :, pl.ds(pl.multiple_of(scol[e] * BS, BS), BS)]
                s1 = fld[srow[e + 1], :, pl.ds(pl.multiple_of(scol[e + 1] * BS, BS), BS)]
                w = w_ref[k, 0:BS, b * BS : (b + 1) * BS].astype(jnp.float32)
                v = w * s0.astype(jnp.float32) + (1.0 - w) * s1.astype(jnp.float32)
                hi, lo = split(v)
                col0 = pl.multiple_of(at * half + b * BS, BS)
                high[pl.ds(row0, BS), pl.ds(col0, BS)] = hi
                low[pl.ds(row0, BS), pl.ds(col0, BS)] = lo
                if first:
                    out = mine_ref if h == 0 else send_ref
                    out[0:BS, b * BS : (b + 1) * BS] = v

    blend_row(0, True)

    @pl.loop(1, n)
    def _(k):
        blend_row(k, False)

    c_hi = ctab[:, 0:MODES]

    @pl.loop(0, n // 2)
    def _(i):
        r0 = pl.multiple_of(i * 2 * BS, 2 * BS)
        rows = pl.ds(r0, 2 * BS)
        a = dot(high[rows, :], ctab[...])
        a = a[:, 0:MODES] + a[:, MODES:] + dot(low[rows, :], c_hi)
        raw = fld[pl.ds(2 * i, 2)].reshape(2 * BS, cols)
        r = dot(raw, ctab[...])
        modes[rows, 0:MODES] = a
        modes[rows, MODES:] = r[:, 0:MODES] + r[:, MODES:]

    m_hi, m_lo = split(modes[...])
    r_hi, r_lo = rtab[0:MODES, :], rtab[MODES:, :]
    total = dot(r_hi, m_hi) + (dot(r_hi, m_lo) + dot(r_lo, m_hi))
    send_ref[BS:, 0 : 2 * MODES] = total


def nudge_kernel(
    per_core, place, coupling, fields, mine, send, recv, driver, relax, rtab, ctab, out_ref
):
    my_col = place[0]
    fields_count = 2 * per_core
    r_hi, r_lo = rtab[:, 0:MODES], rtab[:, MODES:]
    c_hi, c_lo = ctab[0:MODES, :], ctab[MODES:, :]
    raw = []
    for h, ref in ((0, send), (1, recv)):
        at = my_col if h == 0 else 1 - my_col
        for i in range(per_core):
            raw.append((at * per_core + i, ref[i][BS:, MODES : 2 * MODES]))
    index = 0
    for h, ref in ((0, send), (1, recv)):
        for i in range(per_core):
            g = raw[index][0]
            index += 1
            coeff = ref[i][BS:, 0:MODES]
            for f, hat in raw:
                coeff = coeff + coupling[g * fields_count + f] * hat
            term = relax[g] * (driver[g] - coeff)
            t_hi, t_lo = split(term)
            rows = dot(r_hi, t_hi) + (dot(r_hi, t_lo) + dot(r_lo, t_hi))
            a_hi, a_lo = split(rows)
            corr = dot(a_hi, c_hi) + (dot(a_hi, c_lo) + dot(a_lo, c_hi))
            blend = mine[i][...] if h == 0 else ref[i][0:BS, :]
            out_ref[g] = blend + corr

    @pl.loop(0, BS // 16)
    def _(j):
        rows = pl.ds(pl.multiple_of(j * 16, 16), 16)
        x = [fields[f, rows, :].astype(jnp.float32) for f in range(fields_count)]
        for g in range(fields_count):
            acc = coupling[g * fields_count] * x[0]
            for f in range(1, fields_count):
                acc = acc + coupling[g * fields_count + f] * x[f]
            out_ref[g, rows, :] = out_ref[g, rows, :] + acc


def body(ring, fields, weights, source_tile, source_block, coupling, driver, relaxation):
    bf16, f32, i32 = jnp.bfloat16, jnp.float32, jnp.int32
    n = len(ring)
    fields_count, tile_rows, tile_cols = fields.shape
    per_tile = tile_cols // BS
    cols_count = lax.axis_size("tx")
    per_core = fields_count // cols_count
    cols = tile_cols * cols_count
    my_row = lax.axis_index("ty")
    my_col = lax.axis_index("tx")
    swap = [(0, 1), (1, 0)]
    forward = [(ring[i], ring[(i + 1) % n]) for i in range(n)]
    backward = [(b, a) for a, b in forward]
    spot = np.zeros(n, np.int32)
    spot[np.asarray(ring)] = np.arange(n)
    my_spot = jnp.asarray(spot)[my_row]
    place = jnp.asarray(np.asarray(ring, np.int32))[(my_spot - jnp.arange(n)) % n]
    place = jnp.concatenate([place, my_col[None]]).astype(i32)

    def gather(x, up):
        ahead, behind = [], []
        a = b = x
        for i in range(max(up, n - 1 - up)):
            if i < up:
                a = lax.ppermute(a, "ty", forward)
                ahead.append(a)
            if i < n - 1 - up:
                b = lax.ppermute(b, "ty", backward)
                behind.append(b)
        return [x] + ahead + behind[::-1]

    more, fewer = n // 2, n - 1 - n // 2
    ids = jnp.concatenate([source_tile.reshape(-1), source_block.reshape(-1)]).astype(bf16)
    id_rows = jnp.zeros((IDX_ROWS, tile_cols), bf16).at[0, : ids.shape[0]].set(ids)
    w_pieces = gather(jnp.concatenate([weights, id_rows], axis=0), fewer)

    keep = lax.dynamic_slice_in_dim(fields, my_col * per_core, per_core, 0)
    give = lax.dynamic_slice_in_dim(fields, (1 - my_col) * per_core, per_core, 0)
    take = lax.ppermute(give, "tx", swap)
    first = my_col == 0
    strips = []
    for i in range(per_core):
        strips.append(
            jnp.concatenate(
                [jnp.where(first, keep[i], take[i]), jnp.where(first, take[i], keep[i])], axis=1
            )
        )
    f_pieces = [gather(strips[i], more if i % 2 == 0 else fewer) for i in range(per_core)]

    w_own = jnp.stack(w_pieces)
    w_other = lax.ppermute(w_own, "tx", swap)
    requests = per_tile * KSRC
    both = jnp.stack([w_own[:, tile_rows, : 2 * requests], w_other[:, tile_rows, : 2 * requests]], 1)
    both = both.astype(i32)
    tiles, blocks = both[:, :, :requests].reshape(-1), both[:, :, requests:].reshape(-1)
    srow = tiles // cols_count
    scol = tiles % cols_count * per_tile + blocks

    table = wave_table(cols)
    row_table = wave_table(n * tile_rows)
    ctab, rtab = jnp.asarray(table), jnp.asarray(np.ascontiguousarray(row_table.T))
    vmem = pl.BlockSpec(memory_space=pltpu.VMEM)
    smem = pl.BlockSpec(memory_space=pltpu.SMEM)
    area = n * tile_rows * cols
    mine, send = [], []
    for i in range(per_core):
        m, s = pl.pallas_call(
            functools.partial(remap_kernel, n, per_tile, cols),
            out_shape=(
                jax.ShapeDtypeStruct((tile_rows, tile_cols), f32),
                jax.ShapeDtypeStruct((tile_rows + MODES, tile_cols), f32),
            ),
            in_specs=[smem] * 3 + [pl.BlockSpec(memory_space=pl.ANY)] * n + [vmem] * 4,
            out_specs=(vmem, vmem),
            scratch_shapes=[
                pltpu.VMEM((n, tile_rows, cols), bf16),
                pltpu.VMEM((n * tile_rows, cols), bf16),
                pltpu.VMEM((n * tile_rows, cols), bf16),
                pltpu.VMEM((n * tile_rows, 2 * MODES), f32),
                pltpu.SemaphoreType.DMA((n,)),
            ],
            cost_estimate=pl.CostEstimate(
                flops=area * 6 * MODES, bytes_accessed=area * 4, transcendentals=0
            ),
            name="remap",
        )(srow, scol, place, *f_pieces[i], w_own, w_other, ctab, rtab)
        mine.append(m)
        send.append(s)
    recv = [lax.ppermute(s, "tx", swap) for s in send]

    r_here = lax.dynamic_slice_in_dim(jnp.asarray(row_table), my_row * tile_rows, tile_rows, 0)
    c_here = lax.dynamic_slice_in_dim(
        jnp.asarray(np.ascontiguousarray(table.T)), my_col * tile_cols, tile_cols, 1
    )

    def nudge(place_ref, coupling_ref, fields_ref, *refs):
        k = per_core
        nudge_kernel(
            k, place_ref, coupling_ref, fields_ref, refs[:k], refs[k : 2 * k], refs[2 * k : 3 * k],
            *refs[3 * k :],
        )

    return pl.pallas_call(
        nudge,
        out_shape=jax.ShapeDtypeStruct(fields.shape, f32),
        in_specs=[smem] * 2 + [vmem] * (5 + 3 * per_core),
        out_specs=vmem,
        cost_estimate=pl.CostEstimate(
            flops=fields.size * 6 * MODES, bytes_accessed=fields.size * 12, transcendentals=0
        ),
        name="nudge",
    )(
        my_col[None].astype(i32), coupling.astype(f32).reshape(-1), fields, *mine, *send, *recv,
        driver, relaxation, r_here, c_here,
    )


def solution(mesh):
    in_specs = (
        P(None, ("groups", "ty"), "tx"),
        P(("groups", "ty"), "tx"),
        P(("groups", "ty"), "tx", None),
        P(("groups", "ty"), "tx", None),
        P(),
        P(),
        P(),
    )
    out_specs = P(None, ("groups", "ty"), "tx")
    return jax.shard_map(
        functools.partial(body, ring_order(mesh)),
        mesh=mesh, in_specs=in_specs, out_specs=out_specs, check_vma=False,
    )
```
